32 devices in a mesh: dir: 2 (over x), gz: 8 (over z, y), gy: 2 (over core).
Axes of the slice: x: 2, y: 2, z: 4, core: 2. Of those that a mesh axis runs over, the one named last changes fastest.
Arguments:
- estimate: bfloat16 [96, 64, 128, 128], P('dir', 'gz', 'gy'), may hold values from -6 to 6
- observed: bfloat16 [96, 64, 128, 128], P('dir', 'gz', 'gy'), may hold values from -6 to 6
- profile_weight: float32 [17], replicated, may hold values from 0.02 to 0.12
- band_offset: int32 [17], replicated, may hold values from -8 to 8, as said below
- slab_shot: int32 [8], replicated, may hold values from 0 to 3
- shot_gain: float32 [4, 96], P(None, 'dir'), may hold values from 0.1 to 1.9
- fit_matrix: bfloat16 [96, 45], replicated, may hold values from -0.625 to 0.625
- basis: bfloat16 [45, 96], replicated, may hold values from -0.875 to 0.875
Outputs:
- correction: bfloat16 [96, 64, 128, 128], P('dir', 'gz', 'gy')
- updated: bfloat16 [96, 64, 128, 128], P('dir', 'gz', 'gy')
The draws below stay inside these ranges and needn't reach their ends.
Inputs may be any that keep to these rules, and one draw needn't show every extreme that they name: `band_offset`: the first tap's offset is -8 and the last tap's is 8.
All inputs are finite; a program needn't handle non-finite values.
Results may differ from the reference program's by a relative error of at most 0.0055.
Values may be sent and summed in bfloat16 or wider, within the bound.
A program may use at most 128 MiB of HBM per device.

```python
import jax
import jax.numpy as jnp
from jax import lax

NDIR = 96
NCOEF = 45
TAPS = 17
HALO = 8
SLAB = 8
SHOTS = 4
NX = 128
NZ = 64
NY = 128
SLABS = 8


def draw_band_offset(key, part):
    middle = jax.random.randint(key, (TAPS - 2,), -HALO, HALO + 1).astype(jnp.int32)
    first = jnp.full((1,), -HALO, jnp.int32)
    last = jnp.full((1,), HALO, jnp.int32)
    return jnp.concatenate([first, middle, last])


def plant(drawn, rng, smallest, high):
    extent = drawn.shape
    index_at = [jax.random.randint(jax.random.fold_in(rng, axis), (), 0, extent[axis]) for axis in range(len(extent))]
    drawn = drawn.at[tuple(index_at)].set(smallest)
    longest = extent.index(max(extent))
    index_at[longest] = (index_at[longest] + 1) % extent[longest]
    return drawn.at[tuple(index_at)].set(high)


def block_scale(key, dims, pieces, smallest, high):
    level, own = 1.0, jax.random.fold_in(key, 6)
    for dim, shards_of in pieces:
        heights = jnp.exp(jax.random.uniform(jax.random.fold_in(own, dim), (shards_of,), jnp.float32, smallest / len(pieces), high / len(pieces)))
        level = level * jnp.repeat(heights, dims[dim] // shards_of).reshape([-1 if axis == dim else 1 for axis in range(len(dims))])
    return level


def bell_draw(own_key, shape, width, bound, pieces=(), kind=jnp.bfloat16):
    values = jax.random.normal(own_key, shape, jnp.float32) * width
    if len(pieces) > 0:
        values = block_scale(own_key, shape, pieces, -0.22, 0.18) * values
    return jnp.clip(values, min=-bound, max=bound).astype(kind)


def setup_inputs(seed: int = 0) -> dict:
    keys = jax.random.split(jax.random.key(seed), 9)
    return {
        "estimate": bell_draw(keys[0], (NDIR, NZ, NY, NX), 1.0, 6.0, ((0, 2), (1, 8), (2, 2))),
        "observed": bell_draw(keys[1], (NDIR, NZ, NY, NX), 1.0, 6.0, ((0, 2), (1, 8), (2, 2))),
        "profile_weight": jnp.clip(jax.random.uniform(keys[2], (TAPS,), jnp.float32, 0.02, 0.12), 0.02, 0.12),
        "band_offset": draw_band_offset(jax.random.fold_in(keys[8], 71), 0),
        "slab_shot": plant(jax.random.randint(keys[4], (SLABS,), 0, SHOTS), jax.random.fold_in(keys[4], 1), 0, SHOTS - 1).astype(jnp.int32),
        "shot_gain": jnp.clip(1.0 + 0.18 * jax.random.normal(keys[5], (SHOTS, NDIR), jnp.float32), 0.1, 1.9),
        "fit_matrix": bell_draw(keys[6], (NDIR, NCOEF), NDIR ** -0.5, 0.625),
        "basis": bell_draw(keys[7], (NCOEF, NDIR), NCOEF ** -0.5, 0.875),
    }


STEP_SIZE = 0.5


def band_sum(padded, weights, offsets, sign, count, axis):
    total = jnp.zeros(padded.shape[:axis] + (count,) + padded.shape[axis + 1:], jnp.float32)
    for tap in range(TAPS):
        start = (HALO + sign * offsets[tap]).astype(jnp.int32)
        piece = lax.dynamic_slice_in_dim(padded, start, count, axis)
        total = total + weights[tap] * piece.astype(jnp.float32)
    return total


def reference(estimate, observed, profile_weight, band_offset, slab_shot, shot_gain, fit_matrix, basis):
    depth = jnp.arange(NZ, dtype=jnp.int32) // SLAB
    slab_hit = (depth[:, None] == jnp.arange(SLABS, dtype=jnp.int32)[None, :]).astype(jnp.int32)
    shot_of_z = jnp.sum(slab_hit * slab_shot[None, :], axis=1)
    shot_hit = (shot_of_z[:, None] == jnp.arange(SHOTS, dtype=jnp.int32)[None, :]).astype(jnp.float32)
    gain = jnp.sum(shot_hit[:, :, None] * shot_gain[None, :, :], axis=1)

    def one_direction(item):
        volume, seen, scale = item
        padded = jnp.pad(volume.astype(jnp.float32), ((HALO, HALO), (0, 0), (0, 0)))
        blurred = band_sum(padded, profile_weight, band_offset, 1, NZ, 0)
        scale = scale[:, None, None]
        return (scale * (seen.astype(jnp.float32) - scale * blurred)).astype(jnp.bfloat16)

    residual = lax.map(one_direction, (estimate, observed, gain.T))
    by_depth = jnp.moveaxis(residual, 1, 0)

    def fit_depth(rows):
        flat = rows.reshape(NDIR, NY * NX)
        fitted = jnp.dot(fit_matrix.T, flat, preferred_element_type=jnp.float32)
        return fitted.astype(jnp.bfloat16).reshape(NCOEF, NY, NX)

    coeffs = lax.map(fit_depth, by_depth)
    padded = jnp.pad(coeffs.astype(jnp.float32), ((HALO, HALO), (0, 0), (0, 0), (0, 0)))
    filtered = band_sum(padded, profile_weight, band_offset, -1, NZ, 0)
    basis_wide = basis.T.astype(jnp.float32)

    def synth_depth(rows):
        flat = rows.reshape(NCOEF, NY * NX)
        made = jnp.dot(basis_wide, flat, precision=lax.Precision.HIGHEST)
        return made.astype(jnp.bfloat16).reshape(NDIR, NY, NX)

    correction = jnp.moveaxis(lax.map(synth_depth, filtered), 0, 1)
    updated = (estimate.astype(jnp.float32) + STEP_SIZE * correction.astype(jnp.float32)).astype(jnp.bfloat16)
    return (correction, updated)
```

```python
import functools

import jax
import jax.numpy as jnp
from jax import lax
from jax.experimental import pallas as pl
from jax.experimental.pallas import tpu as pltpu
from jax.sharding import PartitionSpec as P

SLAB = 8
STEP_SIZE = 0.5
ROWS = 8
PIECES = 4
CUTS = 2
MESH = pl.DeviceIdType.MESH

def divisor(count, most):
    return max(size for size in range(1, most + 1) if count % size == 0)


def iota(shape, axis):
    return lax.broadcasted_iota(jnp.int32, shape, axis)


def ones_where(hit):
    return jnp.where(hit, 1.0, 0.0).astype(jnp.bfloat16)


def against(a, b):
    return lax.dot_general(a, b, (((1,), (1,)), ((), ())), preferred_element_type=jnp.float32)


def same_row(shape):
    return lax.rem(iota(shape, 0), ROWS) == lax.rem(iota(shape, 1), ROWS)


def band_matrix(weight, offset, odd, depth, sign):
    shape = (2 * depth * ROWS, 4 * depth * ROWS)
    at, source = iota(shape, 0) // ROWS, iota(shape, 1) // ROWS

    def place(block):
        return block + odd * (3 - 2 * block)

    gap = place(source // depth) * depth + lax.rem(source, depth)
    gap = sign * (gap - place(1 + at // depth) * depth - lax.rem(at, depth))
    total = jnp.zeros(shape, jnp.float32)
    for tap in range(weight.shape[0]):
        total = total + jnp.where(gap == offset[tap], weight[tap], 0.0)
    total = jnp.where(same_row(shape), total, 0.0)
    high = total.astype(jnp.bfloat16)
    low = (total - high.astype(jnp.float32)).astype(jnp.bfloat16)
    return jnp.concatenate([high, low], axis=0)


def exchange_kernel(
    sizes, est, obs, weight, offset, shot, gain, fit, out,
    est_kept, obs_kept, est_got, obs_got, far_a, far_b, res, band, band_back, fit_wide, own,
    part_out, part_in, coef, coef_a, coef_b, mine, other, returned,
    load_sem, store_sem, pair_sem, far_sem, part_sem, edge_sem, back_sem, ret_sem,
):
    parts, slabs, chunks, dirs, depth, width, share = sizes
    slab = lax.axis_index("gz").astype(jnp.int32)
    part = lax.axis_index("dir").astype(jnp.int32)
    odd = lax.rem(slab, 2)
    partner = slab + 1 - 2 * odd
    away = slab - 2 + 4 * odd
    across = slab + 2 - 4 * odd
    has_away = jnp.logical_and(away >= 0, away < slabs)
    has_across = jnp.logical_and(across >= 0, across < slabs)
    some = dirs // CUTS
    span = share * ROWS
    count = divisor(share // 2, PIECES)
    step = span // count
    pair_rows = 2 * ROWS
    half = depth * ROWS

    def part_of(hop):
        return lax.rem(part + hop, parts)

    barrier = pltpu.get_barrier_semaphore()

    def greet(name, index):
        pl.semaphore_signal(barrier, inc=1, device_id={name: index}, device_id_type=MESH)

    greet("gz", partner)
    for hop in range(1, parts):
        greet("dir", part_of(hop))

    @pl.when(has_away)
    def _():
        greet("gz", away)

    @pl.when(has_across)
    def _():
        greet("gz", across)

    pl.semaphore_wait(barrier, parts + has_away.astype(jnp.int32) + has_across.astype(jnp.int32))

    def remote(source, target, sems, name, index):
        return pltpu.make_async_remote_copy(
            src_ref=source, dst_ref=target, send_sem=sems.at[0], recv_sem=sems.at[1],
            device_id={name: index}, device_id_type=MESH,
        )

    def rows_at(side, chunk):
        return pl.ds(pl.multiple_of((side * chunks + chunk) * ROWS, ROWS), ROWS)

    def cut_of(cut):
        return pl.ds(cut * some, some)

    def piece(i):
        return pl.ds(i * step, step)

    def pair_copy(kind, chunk, cut):
        source, target = ((est, est_got), (obs, obs_got))[kind]
        return remote(
            source.at[cut_of(cut), :, rows_at(1 - odd, chunk), :],
            target.at[chunk, cut_of(cut)],
            pair_sem.at[kind, chunk, cut], "gz", partner,
        )

    def away_copy(chunk, cut):
        return remote(
            est.at[cut_of(cut), :, rows_at(odd, chunk), :],
            far_a.at[chunk, cut_of(cut)],
            far_sem.at[0, chunk, cut], "gz", away,
        )

    def across_copy(chunk, cut):
        return remote(
            est_got.at[chunk, cut_of(cut)], far_b.at[chunk, cut_of(cut)],
            far_sem.at[1, chunk, cut], "gz", across,
        )

    def load_copy(kind, chunk):
        source, target = ((est, est_kept), (obs, obs_kept))[kind]
        return pltpu.make_async_copy(
            source.at[:, :, rows_at(odd, chunk), :], target.at[chunk], load_sem.at[kind, chunk]
        )

    def part_copy(chunk, hop, i):
        return remote(
            part_out.at[chunk, hop - 1, :, piece(i), :], part_in.at[chunk, hop - 1, :, piece(i), :],
            part_sem.at[chunk, hop - 1, i], "dir", part_of(hop),
        )

    def edge_copy(kind, chunk, i):
        target, index = ((coef_a, away), (coef_b, across))[kind]
        return remote(
            coef.at[chunk, pl.ds(kind * depth, depth), piece(i), :],
            target.at[chunk, :, piece(i), :],
            edge_sem.at[kind, chunk, i], "gz", index,
        )

    def back_copy(chunk, i):
        return remote(
            other.at[chunk, :, piece(i), :], returned.at[chunk, :, piece(i), :],
            back_sem.at[chunk, i], "gz", partner,
        )

    def tile_of(kind, chunk):
        side = odd if kind == 0 else 1 - odd
        return side * chunks + chunk

    def ret_copy(kind, chunk, hop, i):
        source = (mine, returned)[kind]
        return remote(
            source.at[chunk, :, piece(i), :], out.at[tile_of(kind, chunk), part, :, piece(i), :],
            ret_sem.at[kind, chunk, hop - 1, i], "dir", part_of(hop),
        )

    def store_copy(kind, chunk):
        source = (mine, returned)[kind]
        return pltpu.make_async_copy(
            source.at[chunk], out.at[tile_of(kind, chunk), part], store_sem.at[kind, chunk]
        )

    def begin(chunk):
        for kind in range(2):
            for cut in range(CUTS):
                pair_copy(kind, chunk, cut).start()

        @pl.when(has_away)
        def _():
            for cut in range(CUTS):
                away_copy(chunk, cut).start()

        for kind in range(2):
            load_copy(kind, chunk).start()

    def forward(chunk, cut):
        pair_copy(0, chunk, cut).wait_recv()

        @pl.when(has_across)
        def _():
            across_copy(chunk, cut).start()

    def arrive(near, far):
        @pl.when(has_across)
        def _():
            near.wait_recv()

        @pl.when(has_away)
        def _():
            far.wait_recv()

    shots = [shot[lax.div(index * depth, SLAB)] for index in (slab, partner)]

    def residual(chunk, cut):
        arrive(away_copy(chunk, cut), across_copy(chunk, cut))
        pair_copy(1, chunk, cut).wait_recv()

        def one(j, carry):
            d = cut * some + 2 * j
            columns = []
            for e in range(2):
                planes = [
                    ref[chunk, d + e].astype(jnp.float32).reshape(half, width)
                    for ref in (far_b, est_kept, est_got, far_a)
                ]
                columns.append(jnp.concatenate(planes, axis=0))
            wide = jnp.concatenate(columns, axis=1).astype(jnp.bfloat16)
            sums = jnp.dot(band[...], wide, preferred_element_type=jnp.float32)
            sums = sums[: 2 * half] + sums[2 * half :]
            for o, seen in enumerate((obs_kept, obs_got)):
                values = []
                for e in range(2):
                    scale = gain[shots[o], d + e]
                    blurred = sums[o * half : (o + 1) * half, e * width : (e + 1) * width]
                    value = seen[chunk, d + e].astype(jnp.float32).reshape(half, width)
                    values.append(scale * (value - scale * blurred))
                at = pl.ds(pl.multiple_of(d * ROWS, pair_rows), pair_rows)
                for z in range(depth):
                    cut_rows = slice(z * ROWS, (z + 1) * ROWS)
                    both = jnp.concatenate([value[cut_rows] for value in values], axis=0)
                    res[o * depth + z, at, :] = both.astype(jnp.bfloat16)
            return carry

        lax.fori_loop(0, some // 2, one, 0)

    def fitting(chunk):
        def one(j, carry):
            z = 2 * j
            wide = jnp.concatenate([res[z], res[z + 1]], axis=1)
            made = jnp.dot(fit_wide[...], wide, preferred_element_type=jnp.float32)
            for e in range(2):
                value = made[:, e * width : (e + 1) * width]
                own[z + e] = value[:span]
                for hop in range(1, parts):
                    piece_of = value[hop * span : (hop + 1) * span]
                    part_out[chunk, hop - 1, z + e] = piece_of.astype(jnp.bfloat16)
            return carry

        lax.fori_loop(0, depth, one, 0)
        for i in range(count):
            for hop in range(1, parts):
                part_copy(chunk, hop, i).start()

    def gather(chunk, i):
        for hop in range(1, parts):
            part_copy(chunk, hop, i).wait_recv()

        def one(z, carry):
            value = own[z, piece(i), :]
            for hop in range(1, parts):
                value = value + part_in[chunk, hop - 1, z, piece(i), :].astype(jnp.float32)
            coef[chunk, z, piece(i), :] = value.astype(jnp.bfloat16)
            return carry

        lax.fori_loop(0, 2 * depth, one, 0)

        @pl.when(has_away)
        def _():
            edge_copy(0, chunk, i).start()

        @pl.when(has_across)
        def _():
            edge_copy(1, chunk, i).start()

    def smooth(chunk, i):
        arrive(edge_copy(0, chunk, i), edge_copy(1, chunk, i))

        def one(j, carry):
            at = pl.ds(pl.multiple_of(i * step + j * pair_rows, pair_rows), pair_rows)
            planes = [coef_b[chunk, z, at, :] for z in range(depth)]
            planes += [coef[chunk, z, at, :] for z in range(2 * depth)]
            planes += [coef_a[chunk, z, at, :] for z in range(depth)]
            planes = [plane.astype(jnp.float32) for plane in planes]
            columns = [
                jnp.concatenate([plane[e * ROWS : (e + 1) * ROWS] for plane in planes], axis=0)
                for e in range(2)
            ]
            wide = jnp.concatenate(columns, axis=1).astype(jnp.bfloat16)
            sums = jnp.dot(band_back[...], wide, preferred_element_type=jnp.float32)
            sums = sums[: 2 * half] + sums[2 * half :]
            for o, ref in enumerate((mine, other)):
                for z in range(depth):
                    value = sums[o * half + z * ROWS : o * half + (z + 1) * ROWS]
                    both = jnp.concatenate([value[:, :width], value[:, width:]], axis=0)
                    ref[chunk, z, at, :] = both.astype(jnp.bfloat16)
            return carry

        lax.fori_loop(0, step // pair_rows, one, 0)
        back_copy(chunk, i).start()
        for hop in range(1, parts):
            ret_copy(0, chunk, hop, i).start()

    def pass_on(chunk, i):
        back_copy(chunk, i).wait_recv()
        for hop in range(1, parts):
            ret_copy(1, chunk, hop, i).start()

    begin(0)
    if chunks > 1:
        begin(1)

    nothing = jnp.zeros((dirs, depth, ROWS, width), jnp.bfloat16)
    no_coef = jnp.zeros((depth, span, width), jnp.bfloat16)

    def clear(ref, value):
        def one(chunk, carry):
            ref[chunk] = value
            return carry

        lax.fori_loop(0, chunks, one, 0)

    @pl.when(jnp.logical_not(has_across))
    def _():
        clear(far_a, nothing)
        clear(coef_a, no_coef)

    @pl.when(jnp.logical_not(has_away))
    def _():
        clear(far_b, nothing)
        clear(coef_b, no_coef)

    band[...] = band_matrix(weight, offset, odd, depth, 1)
    band_back[...] = band_matrix(weight, offset, odd, depth, -1)
    line = iota((parts * span, fit.shape[1]), 0) // ROWS
    chosen = lax.rem(line // share + part, parts) * share + lax.rem(line, share)
    spread = ones_where(chosen == iota(line.shape, 1))
    narrow = against(spread, fit[...]).astype(jnp.bfloat16)
    shape = (dirs * ROWS, fit.shape[0])
    spread = ones_where(iota(shape, 0) // ROWS + part * dirs == iota(shape, 1))
    full = against(narrow, spread)
    fit_wide[...] = jnp.where(same_row(full.shape), full, 0.0).astype(jnp.bfloat16)

    for cut in range(CUTS):
        forward(0, cut)
    for chunk in range(chunks):
        more = chunk + 1 < chunks
        for kind in range(2):
            load_copy(kind, chunk).wait()
        for cut in range(CUTS):
            residual(chunk, cut)
        fitting(chunk)
        if chunk:
            for i in range(count):
                pass_on(chunk - 1, i)
            store_copy(1, chunk - 1).start()
        for i in range(count):
            gather(chunk, i)
            for cut in range(CUTS):
                if more and cut * count // CUTS == i:
                    forward(chunk + 1, cut)
            if i:
                smooth(chunk, i - 1)
            if not more and i > 1:
                pass_on(chunk, i - 2)
        smooth(chunk, count - 1)
        store_copy(0, chunk).start()
        if not more:
            for i in range(max(count - 2, 0), count):
                pass_on(chunk, i)
            store_copy(1, chunk).start()
        if chunk + 2 < chunks:
            begin(chunk + 2)

    for chunk in range(chunks):
        for cut in range(CUTS):
            for kind in range(2):
                pair_copy(kind, chunk, cut).wait_send()

            @pl.when(has_away)
            def _(chunk=chunk, cut=cut):
                away_copy(chunk, cut).wait_send()

            @pl.when(has_across)
            def _(chunk=chunk, cut=cut):
                across_copy(chunk, cut).wait_send()

        for i in range(count):
            for hop in range(1, parts):
                part_copy(chunk, hop, i).wait_send()

            @pl.when(has_away)
            def _(chunk=chunk, i=i):
                edge_copy(0, chunk, i).wait_send()

            @pl.when(has_across)
            def _(chunk=chunk, i=i):
                edge_copy(1, chunk, i).wait_send()

            back_copy(chunk, i).wait_send()
            for kind in range(2):
                for hop in range(1, parts):
                    ret_copy(kind, chunk, hop, i).wait()
        for kind in range(2):
            store_copy(kind, chunk).wait()


def exchange_call(sizes, est, obs, weight, offset, shot, gain, fit):
    parts, slabs, chunks, dirs, depth, width, share = sizes
    span = share * ROWS
    count = divisor(share // 2, PIECES)
    bf16 = jnp.bfloat16
    field = pltpu.VMEM((chunks, dirs, depth, ROWS, width), bf16)
    hops = pltpu.VMEM((chunks, parts - 1, 2 * depth, span, width), bf16)
    edge = pltpu.VMEM((chunks, depth, span, width), bf16)
    square = pltpu.VMEM((4 * depth * ROWS, 4 * depth * ROWS), bf16)
    smem = pl.BlockSpec(memory_space=pltpu.SMEM)
    hbm = pl.BlockSpec(memory_space=pl.ANY)
    dma = pltpu.SemaphoreType.DMA
    return pl.pallas_call(
        functools.partial(exchange_kernel, sizes),
        in_specs=[hbm, hbm, smem, smem, smem, smem, pl.BlockSpec(memory_space=pltpu.VMEM)],
        out_specs=hbm,
        out_shape=jax.ShapeDtypeStruct((2 * chunks, parts, depth, span, width), bf16),
        scratch_shapes=[field] * 6
        + [
            pltpu.VMEM((2 * depth, dirs * ROWS, width), bf16),
            square,
            square,
            pltpu.VMEM((parts * span, dirs * ROWS), bf16),
            pltpu.VMEM((2 * depth, span, width), jnp.float32),
            hops,
            hops,
            pltpu.VMEM((chunks, 2 * depth, span, width), bf16),
        ]
        + [edge] * 5
        + [
            dma((2, chunks)),
            dma((2, chunks)),
            dma((2, chunks, CUTS, 2)),
            dma((2, chunks, CUTS, 2)),
            dma((chunks, parts - 1, count, 2)),
            dma((2, chunks, count, 2)),
            dma((chunks, count, 2)),
            dma((2, chunks, parts - 1, count, 2)),
        ],
        compiler_params=pltpu.CompilerParams(
            collective_id=0, has_side_effects=True, vmem_limit_bytes=60 * 1024 * 1024
        ),
    )(est, obs, weight, offset, shot, gain, fit)


def synthesis_kernel(filtered, estimate, basis, correction, updated, wide):
    parts, depth, span, width = filtered.shape[1:]
    dirs = estimate.shape[0]
    part = lax.axis_index("dir").astype(jnp.int32)

    @pl.when(pl.program_id(0) == 0)
    def _():
        shape = (dirs * ROWS, basis.shape[1])
        spread = ones_where(iota(shape, 0) // ROWS + part * dirs == iota(shape, 1))
        narrow = against(spread, basis[...]).astype(jnp.bfloat16)
        shape = (parts * span, basis.shape[0])
        spread = ones_where(iota(shape, 0) // ROWS == iota(shape, 1))
        full = against(narrow, spread)
        wide[...] = jnp.where(same_row(full.shape), full, 0.0).astype(jnp.bfloat16)

    def one(j, carry):
        z = 2 * j
        columns = [
            jnp.concatenate([filtered[0, p, z + e] for p in range(parts)], axis=0) for e in range(2)
        ]
        made = jnp.dot(
            wide[...], jnp.concatenate(columns, axis=1), preferred_element_type=jnp.float32
        )
        for e in range(2):
            value = made[:, e * width : (e + 1) * width].reshape(dirs, ROWS, width)
            value = value.astype(jnp.bfloat16)
            correction[:, z + e] = value
            updated[:, z + e] = (
                estimate[:, z + e].astype(jnp.float32) + STEP_SIZE * value.astype(jnp.float32)
            ).astype(updated.dtype)
        return carry

    lax.fori_loop(0, depth // 2, one, 0)


def synthesis_call(filtered, estimate, basis):
    tiles, parts, depth, span, width = filtered.shape
    dirs = estimate.shape[0]
    place = pl.BlockSpec((dirs, depth, ROWS, width), lambda i: (0, 0, i, 0))
    shape = jax.ShapeDtypeStruct(estimate.shape, estimate.dtype)
    return pl.pallas_call(
        synthesis_kernel,
        grid=(tiles,),
        in_specs=[
            pl.BlockSpec((1, parts, depth, span, width), lambda i: (i, 0, 0, 0, 0)),
            place,
            pl.BlockSpec(basis.shape, lambda i: (0, 0)),
        ],
        out_specs=[place, place],
        out_shape=[shape, shape],
        scratch_shapes=[pltpu.VMEM((dirs * ROWS, parts * span), jnp.bfloat16)],
    )(filtered, estimate, basis)


def shards(
    estimate, observed, profile_weight, band_offset, slab_shot, shot_gain, fit_matrix, basis
):
    dirs, depth, rows, width = estimate.shape
    parts = lax.axis_size("dir")
    share = 2 * -(-fit_matrix.shape[1] // (2 * parts))
    sizes = (parts, lax.axis_size("gz"), rows // (2 * ROWS), dirs, depth, width, share)
    filtered = exchange_call(
        sizes, estimate, observed, profile_weight, band_offset, slab_shot, shot_gain, fit_matrix
    )
    return tuple(synthesis_call(filtered, estimate, basis))


def solution(mesh):
    return jax.shard_map(
        shards,
        mesh=mesh,
        in_specs=(
            P("dir", "gz", "gy", None),
            P("dir", "gz", "gy", None),
            P(),
            P(),
            P(),
            P(None, "dir"),
            P(),
            P(),
        ),
        out_specs=(P("dir", "gz", "gy", None), P("dir", "gz", "gy", None)),
        check_vma=False,
    )
```

```python
import functools

import jax
import jax.numpy as jnp
from jax import lax
from jax.experimental import pallas as pl
from jax.experimental.pallas import tpu as pltpu
from jax.sharding import PartitionSpec as P

SLAB = 8
STEP_SIZE = 0.5
ROWS = 8
PIECES = 4
CUTS = 4
MESH = pl.DeviceIdType.MESH

def divisor(count, most):
    return max(size for size in range(1, most + 1) if count % size == 0)


def iota(shape, axis):
    return lax.broadcasted_iota(jnp.int32, shape, axis)


def ones_where(hit):
    return jnp.where(hit, 1.0, 0.0).astype(jnp.bfloat16)


def against(a, b):
    return lax.dot_general(a, b, (((1,), (1,)), ((), ())), preferred_element_type=jnp.float32)


def same_row(shape):
    return lax.rem(iota(shape, 0), ROWS) == lax.rem(iota(shape, 1), ROWS)


def band_matrix(weight, offset, odd, depth, sign):
    shape = (2 * depth * ROWS, 4 * depth * ROWS)
    at, source = iota(shape, 0) // ROWS, iota(shape, 1) // ROWS

    def place(block):
        return block + odd * (3 - 2 * block)

    gap = place(source // depth) * depth + lax.rem(source, depth)
    gap = sign * (gap - place(1 + at // depth) * depth - lax.rem(at, depth))
    total = jnp.zeros(shape, jnp.float32)
    for tap in range(weight.shape[0]):
        total = total + jnp.where(gap == offset[tap], weight[tap], 0.0)
    total = jnp.where(same_row(shape), total, 0.0)
    high = total.astype(jnp.bfloat16)
    low = (total - high.astype(jnp.float32)).astype(jnp.bfloat16)
    half = depth * ROWS
    sides = [piece[o * half : (o + 1) * half] for o in range(2) for piece in (high, low)]
    return jnp.concatenate(sides, axis=0)


def both_parts(sums, half):
    return sums[:half] + sums[half : 2 * half]


def exchange_kernel(
    sizes, est, obs, weight, offset, shot, gain, fit, out,
    fit_kept, est_kept, obs_kept, est_got, obs_got, far_a, far_b, res, band, band_back, fit_wide, own,
    part_out, part_in, coef, coef_a, coef_b, mine, other, returned,
    load_sem, store_sem, pair_sem, far_sem, part_sem, edge_sem, back_sem, ret_sem,
):
    parts, slabs, chunks, dirs, depth, width, share = sizes
    slab = lax.axis_index("gz").astype(jnp.int32)
    part = lax.axis_index("dir").astype(jnp.int32)
    odd = lax.rem(slab, 2)
    partner = slab + 1 - 2 * odd
    away = slab - 2 + 4 * odd
    across = slab + 2 - 4 * odd
    has_away = jnp.logical_and(away >= 0, away < slabs)
    has_across = jnp.logical_and(across >= 0, across < slabs)
    cuts = divisor(dirs // 2, CUTS)
    some = dirs // cuts
    span = share * ROWS
    count = divisor(share // 2, PIECES)
    step = span // count
    pair_rows = 2 * ROWS
    half = depth * ROWS

    def part_of(hop):
        return lax.rem(part + hop, parts)

    barrier = pltpu.get_barrier_semaphore()

    def greet(name, index):
        pl.semaphore_signal(barrier, inc=1, device_id={name: index}, device_id_type=MESH)

    greet("gz", partner)
    for hop in range(1, parts):
        greet("dir", part_of(hop))

    @pl.when(has_away)
    def _():
        greet("gz", away)

    @pl.when(has_across)
    def _():
        greet("gz", across)

    pl.semaphore_wait(barrier, parts + has_away.astype(jnp.int32) + has_across.astype(jnp.int32))

    def remote(source, target, sems, name, index):
        return pltpu.make_async_remote_copy(
            src_ref=source, dst_ref=target, send_sem=sems.at[0], recv_sem=sems.at[1],
            device_id={name: index}, device_id_type=MESH,
        )

    def rows_at(side, chunk):
        return pl.ds(pl.multiple_of((side * chunks + chunk) * ROWS, ROWS), ROWS)

    def cut_of(cut):
        return pl.ds(cut * some, some)

    def piece(i):
        return pl.ds(i * step, step)

    def pair_copy(kind, chunk, cut):
        source, target = ((est, est_got), (obs, obs_got))[kind]
        return remote(
            source.at[cut_of(cut), :, rows_at(1 - odd, chunk), :],
            target.at[chunk, cut_of(cut)],
            pair_sem.at[kind, chunk, cut], "gz", partner,
        )

    def away_copy(chunk, cut):
        return remote(
            est.at[cut_of(cut), :, rows_at(odd, chunk), :],
            far_a.at[chunk, cut_of(cut)],
            far_sem.at[0, chunk, cut], "gz", away,
        )

    def across_copy(chunk, cut):
        return remote(
            est_got.at[chunk, cut_of(cut)], far_b.at[chunk, cut_of(cut)],
            far_sem.at[1, chunk, cut], "gz", across,
        )

    def load_copy(kind, chunk):
        source, target = ((est, est_kept), (obs, obs_kept))[kind]
        return pltpu.make_async_copy(
            source.at[:, :, rows_at(odd, chunk), :], target.at[chunk], load_sem.at[kind, chunk]
        )

    def part_copy(o, chunk, hop, i):
        at = (chunk, hop - 1, pl.ds(o * depth, depth), piece(i))
        return remote(
            part_out.at[at], part_in.at[at], part_sem.at[o, chunk, hop - 1, i], "dir", part_of(hop)
        )

    def edge_copy(kind, chunk, i):
        target, index = ((coef_a, away), (coef_b, across))[kind]
        return remote(
            coef.at[chunk, pl.ds(kind * depth, depth), piece(i), :],
            target.at[chunk, :, piece(i), :],
            edge_sem.at[kind, chunk, i], "gz", index,
        )

    def back_copy(chunk, i):
        return remote(
            other.at[chunk, :, piece(i), :], returned.at[chunk, :, piece(i), :],
            back_sem.at[chunk, i], "gz", partner,
        )

    def tile_of(kind, chunk):
        side = odd if kind == 0 else 1 - odd
        return side * chunks + chunk

    def ret_copy(kind, chunk, hop, i):
        source = (mine, returned)[kind]
        return remote(
            source.at[chunk, :, piece(i), :], out.at[tile_of(kind, chunk), part, :, piece(i), :],
            ret_sem.at[kind, chunk, hop - 1, i], "dir", part_of(hop),
        )

    def store_copy(kind, chunk):
        source = (mine, returned)[kind]
        return pltpu.make_async_copy(
            source.at[chunk], out.at[tile_of(kind, chunk), part], store_sem.at[kind, chunk]
        )

    def begin(chunk):
        for kind in range(2):
            for cut in range(cuts):
                pair_copy(kind, chunk, cut).start()

        @pl.when(has_away)
        def _():
            for cut in range(cuts):
                away_copy(chunk, cut).start()

        for kind in range(2):
            load_copy(kind, chunk).start()

    def forward(chunk, cut):
        pair_copy(0, chunk, cut).wait_recv()

        @pl.when(has_across)
        def _():
            across_copy(chunk, cut).start()

    def arrive(near, far):
        @pl.when(has_across)
        def _():
            near.wait_recv()

        @pl.when(has_away)
        def _():
            far.wait_recv()

    shots = [shot[lax.div(index * depth, SLAB)] for index in (slab, partner)]

    def residual(o, chunk, cut):
        if o:
            pair_copy(1, chunk, cut).wait_recv()
        else:
            arrive(away_copy(chunk, cut), across_copy(chunk, cut))
        seen = (obs_kept, obs_got)[o]

        def one(j, carry):
            d = cut * some + 2 * j
            columns = []
            for e in range(2):
                planes = [
                    ref[chunk, d + e].astype(jnp.float32).reshape(half, width)
                    for ref in (far_b, est_kept, est_got, far_a)
                ]
                columns.append(jnp.concatenate(planes, axis=0))
            wide = jnp.concatenate(columns, axis=1).astype(jnp.bfloat16)
            rows = band[2 * o * half : 2 * (o + 1) * half, :]
            sums = both_parts(jnp.dot(rows, wide, preferred_element_type=jnp.float32), half)
            values = []
            for e in range(2):
                scale = gain[shots[o], d + e]
                value = seen[chunk, d + e].astype(jnp.float32).reshape(half, width)
                value = value - scale * sums[:, e * width : (e + 1) * width]
                values.append(scale * value)
            at = pl.ds(pl.multiple_of(d * ROWS, pair_rows), pair_rows)
            for z in range(depth):
                cut_rows = slice(z * ROWS, (z + 1) * ROWS)
                both = jnp.concatenate([value[cut_rows] for value in values], axis=0)
                res[o * depth + z, at, :] = both.astype(jnp.bfloat16)
            return carry

        lax.fori_loop(0, some // 2, one, 0)

    def fitting(o, chunk):
        def one(j, carry):
            z = o * depth + 2 * j
            wide = jnp.concatenate([res[z], res[z + 1]], axis=1)
            made = jnp.dot(fit_wide[...], wide, preferred_element_type=jnp.float32)
            for e in range(2):
                value = made[:, e * width : (e + 1) * width]
                own[z + e] = value[:span]
                for hop in range(1, parts):
                    piece_of = value[hop * span : (hop + 1) * span]
                    part_out[chunk, hop - 1, z + e] = piece_of.astype(jnp.bfloat16)
            return carry

        lax.fori_loop(0, depth // 2, one, 0)
        for i in range(count):
            for hop in range(1, parts):
                part_copy(o, chunk, hop, i).start()

    def gather(o, chunk, i):
        for hop in range(1, parts):
            part_copy(o, chunk, hop, i).wait_recv()

        def one(z, carry):
            value = own[z, piece(i), :]
            for hop in range(1, parts):
                value = value + part_in[chunk, hop - 1, z, piece(i), :].astype(jnp.float32)
            coef[chunk, z, piece(i), :] = value.astype(jnp.bfloat16)
            return carry

        lax.fori_loop(o * depth, (o + 1) * depth, one, 0)

        @pl.when((has_away, has_across)[o])
        def _():
            edge_copy(o, chunk, i).start()

    def smooth(chunk, i):
        arrive(edge_copy(0, chunk, i), edge_copy(1, chunk, i))

        def one(j, carry):
            at = pl.ds(pl.multiple_of(i * step + j * pair_rows, pair_rows), pair_rows)
            planes = [coef_b[chunk, z, at, :] for z in range(depth)]
            planes += [coef[chunk, z, at, :] for z in range(2 * depth)]
            planes += [coef_a[chunk, z, at, :] for z in range(depth)]
            planes = [plane.astype(jnp.float32) for plane in planes]
            columns = [
                jnp.concatenate([plane[e * ROWS : (e + 1) * ROWS] for plane in planes], axis=0)
                for e in range(2)
            ]
            wide = jnp.concatenate(columns, axis=1).astype(jnp.bfloat16)
            sums = jnp.dot(band_back[...], wide, preferred_element_type=jnp.float32)
            for o, ref in enumerate((mine, other)):
                side = both_parts(sums[2 * o * half : 2 * (o + 1) * half], half)
                for z in range(depth):
                    value = side[z * ROWS : (z + 1) * ROWS]
                    both = jnp.concatenate([value[:, :width], value[:, width:]], axis=0)
                    ref[chunk, z, at, :] = both.astype(jnp.bfloat16)
            return carry

        lax.fori_loop(0, step // pair_rows, one, 0)
        back_copy(chunk, i).start()
        for hop in range(1, parts):
            ret_copy(0, chunk, hop, i).start()

    def pass_on(chunk, i):
        back_copy(chunk, i).wait_recv()
        for hop in range(1, parts):
            ret_copy(1, chunk, hop, i).start()

    fit_copy = pltpu.make_async_copy(fit, fit_kept, load_sem.at[2, 0])
    fit_copy.start()
    begin(0)
    if chunks > 1:
        begin(1)

    nothing = jnp.zeros((dirs, depth, ROWS, width), jnp.bfloat16)
    no_coef = jnp.zeros((depth, span, width), jnp.bfloat16)

    def clear(ref, value):
        def one(chunk, carry):
            ref[chunk] = value
            return carry

        lax.fori_loop(0, chunks, one, 0)

    @pl.when(jnp.logical_not(has_across))
    def _():
        clear(far_a, nothing)
        clear(coef_a, no_coef)

    @pl.when(jnp.logical_not(has_away))
    def _():
        clear(far_b, nothing)
        clear(coef_b, no_coef)

    band[...] = band_matrix(weight, offset, odd, depth, 1)
    band_back[...] = band_matrix(weight, offset, odd, depth, -1)
    line = iota((parts * span, fit.shape[0]), 0) // ROWS
    chosen = lax.rem(line // share + part, parts) * share + lax.rem(line, share)
    spread = ones_where(chosen == iota(line.shape, 1))
    fit_copy.wait()
    narrow = jnp.dot(spread, fit_kept[...], preferred_element_type=jnp.float32).astype(jnp.bfloat16)
    shape = (dirs * ROWS, fit.shape[1])
    spread = ones_where(iota(shape, 0) // ROWS + part * dirs == iota(shape, 1))
    full = against(narrow, spread)
    fit_wide[...] = jnp.where(same_row(full.shape), full, 0.0).astype(jnp.bfloat16)

    for cut in range(cuts):
        forward(0, cut)
    for chunk in range(chunks):
        more = chunk + 1 < chunks
        for kind in range(2):
            load_copy(kind, chunk).wait()
        for cut in range(cuts):
            residual(0, chunk, cut)
        fitting(0, chunk)
        for cut in range(cuts):
            residual(1, chunk, cut)
        fitting(1, chunk)
        if chunk:
            for i in range(count):
                pass_on(chunk - 1, i)
            store_copy(1, chunk - 1).start()
        for i in range(count):
            gather(0, chunk, i)
        for i in range(count):
            gather(1, chunk, i)
            for cut in range(cuts):
                if more and cut * count // cuts == i:
                    forward(chunk + 1, cut)
            if i:
                smooth(chunk, i - 1)
            if not more and i > 1:
                pass_on(chunk, i - 2)
        smooth(chunk, count - 1)
        store_copy(0, chunk).start()
        if not more:
            for i in range(max(count - 2, 0), count):
                pass_on(chunk, i)
            store_copy(1, chunk).start()
        if chunk + 2 < chunks:
            begin(chunk + 2)

    for chunk in range(chunks):
        for cut in range(cuts):
            for kind in range(2):
                pair_copy(kind, chunk, cut).wait_send()

            @pl.when(has_away)
            def _(chunk=chunk, cut=cut):
                away_copy(chunk, cut).wait_send()

            @pl.when(has_across)
            def _(chunk=chunk, cut=cut):
                across_copy(chunk, cut).wait_send()

        for i in range(count):
            for hop in range(1, parts):
                for o in range(2):
                    part_copy(o, chunk, hop, i).wait_send()

            @pl.when(has_away)
            def _(chunk=chunk, i=i):
                edge_copy(0, chunk, i).wait_send()

            @pl.when(has_across)
            def _(chunk=chunk, i=i):
                edge_copy(1, chunk, i).wait_send()

            back_copy(chunk, i).wait_send()
            for kind in range(2):
                for hop in range(1, parts):
                    ret_copy(kind, chunk, hop, i).wait()
        for kind in range(2):
            store_copy(kind, chunk).wait()


def exchange_call(sizes, est, obs, weight, offset, shot, gain, fit):
    parts, slabs, chunks, dirs, depth, width, share = sizes
    span = share * ROWS
    count = divisor(share // 2, PIECES)
    cuts = divisor(dirs // 2, CUTS)
    bf16 = jnp.bfloat16
    field = pltpu.VMEM((chunks, dirs, depth, ROWS, width), bf16)
    hops = pltpu.VMEM((chunks, parts - 1, 2 * depth, span, width), bf16)
    edge = pltpu.VMEM((chunks, depth, span, width), bf16)
    square = pltpu.VMEM((4 * depth * ROWS, 4 * depth * ROWS), bf16)
    smem = pl.BlockSpec(memory_space=pltpu.SMEM)
    hbm = pl.BlockSpec(memory_space=pl.ANY)
    dma = pltpu.SemaphoreType.DMA
    return pl.pallas_call(
        functools.partial(exchange_kernel, sizes),
        in_specs=[hbm, hbm, smem, smem, smem, smem, hbm],
        out_specs=hbm,
        out_shape=jax.ShapeDtypeStruct((2 * chunks, parts, depth, span, width), bf16),
        scratch_shapes=[pltpu.VMEM(fit.shape[::-1], bf16)]
        + [field] * 6
        + [
            pltpu.VMEM((2 * depth, dirs * ROWS, width), bf16),
            square,
            square,
            pltpu.VMEM((parts * span, dirs * ROWS), bf16),
            pltpu.VMEM((2 * depth, span, width), jnp.float32),
            hops,
            hops,
            pltpu.VMEM((chunks, 2 * depth, span, width), bf16),
        ]
        + [edge] * 5
        + [
            dma((3, chunks)),
            dma((2, chunks)),
            dma((2, chunks, cuts, 2)),
            dma((2, chunks, cuts, 2)),
            dma((2, chunks, parts - 1, count, 2)),
            dma((2, chunks, count, 2)),
            dma((chunks, count, 2)),
            dma((2, chunks, parts - 1, count, 2)),
        ],
        compiler_params=pltpu.CompilerParams(
            collective_id=0, has_side_effects=True, vmem_limit_bytes=60 * 1024 * 1024
        ),
    )(est, obs, weight, offset, shot, gain, fit.T)


def synthesis_kernel(filtered, estimate, basis, correction, updated, wide):
    parts, depth, span, width = filtered.shape[1:]
    dirs = estimate.shape[0]
    part = lax.axis_index("dir").astype(jnp.int32)

    @pl.when(pl.program_id(0) == 0)
    def _():
        shape = (dirs * ROWS, basis.shape[1])
        spread = ones_where(iota(shape, 0) // ROWS + part * dirs == iota(shape, 1))
        narrow = against(spread, basis[...]).astype(jnp.bfloat16)
        shape = (parts * span, basis.shape[0])
        spread = ones_where(iota(shape, 0) // ROWS == iota(shape, 1))
        full = against(narrow, spread)
        wide[...] = jnp.where(same_row(full.shape), full, 0.0).astype(jnp.bfloat16)

    def one(j, carry):
        z = 2 * j
        columns = [
            jnp.concatenate([filtered[0, p, z + e] for p in range(parts)], axis=0) for e in range(2)
        ]
        made = jnp.dot(
            wide[...], jnp.concatenate(columns, axis=1), preferred_element_type=jnp.float32
        )
        for e in range(2):
            value = made[:, e * width : (e + 1) * width].reshape(dirs, ROWS, width)
            value = value.astype(jnp.bfloat16)
            correction[:, z + e] = value
            updated[:, z + e] = (
                estimate[:, z + e].astype(jnp.float32) + STEP_SIZE * value.astype(jnp.float32)
            ).astype(updated.dtype)
        return carry

    lax.fori_loop(0, depth // 2, one, 0)


def synthesis_call(filtered, estimate, basis):
    tiles, parts, depth, span, width = filtered.shape
    dirs = estimate.shape[0]
    place = pl.BlockSpec((dirs, depth, ROWS, width), lambda i: (0, 0, i, 0))
    shape = jax.ShapeDtypeStruct(estimate.shape, estimate.dtype)
    return pl.pallas_call(
        synthesis_kernel,
        grid=(tiles,),
        in_specs=[
            pl.BlockSpec((1, parts, depth, span, width), lambda i: (i, 0, 0, 0, 0)),
            place,
            pl.BlockSpec(basis.shape, lambda i: (0, 0)),
        ],
        out_specs=[place, place],
        out_shape=[shape, shape],
        scratch_shapes=[pltpu.VMEM((dirs * ROWS, parts * span), jnp.bfloat16)],
    )(filtered, estimate, basis)


def shards(
    estimate, observed, profile_weight, band_offset, slab_shot, shot_gain, fit_matrix, basis
):
    dirs, depth, rows, width = estimate.shape
    parts = lax.axis_size("dir")
    share = 2 * -(-fit_matrix.shape[1] // (2 * parts))
    sizes = (parts, lax.axis_size("gz"), rows // (2 * ROWS), dirs, depth, width, share)
    filtered = exchange_call(
        sizes, estimate, observed, profile_weight, band_offset, slab_shot, shot_gain, fit_matrix
    )
    return tuple(synthesis_call(filtered, estimate, basis))


def solution(mesh):
    return jax.shard_map(
        shards,
        mesh=mesh,
        in_specs=(
            P("dir", "gz", "gy", None),
            P("dir", "gz", "gy", None),
            P(),
            P(),
            P(),
            P(None, "dir"),
            P(),
            P(),
        ),
        out_specs=(P("dir", "gz", "gy", None), P("dir", "gz", "gy", None)),
        check_vma=False,
    )
```

```python
import functools

import jax
import jax.numpy as jnp
from jax import lax
from jax.experimental import pallas as pl
from jax.experimental.pallas import tpu as pltpu
from jax.sharding import PartitionSpec as P

SLAB = 8
STEP_SIZE = 0.5
ROWS = 8
PIECES = 4
CUTS = 4
MESH = pl.DeviceIdType.MESH

def divisor(count, most):
    return max(size for size in range(1, most + 1) if count % size == 0)


def iota(shape, axis):
    return lax.broadcasted_iota(jnp.int32, shape, axis)


def ones_where(hit):
    return jnp.where(hit, 1.0, 0.0).astype(jnp.bfloat16)


def against(a, b):
    return lax.dot_general(a, b, (((1,), (1,)), ((), ())), preferred_element_type=jnp.float32)


def same_row(shape):
    return lax.rem(iota(shape, 0), ROWS) == lax.rem(iota(shape, 1), ROWS)


def band_matrix(weight, offset, odd, depth, sign):
    shape = (2 * depth * ROWS, 4 * depth * ROWS)
    at, source = iota(shape, 0) // ROWS, iota(shape, 1) // ROWS

    def place(block):
        return block + odd * (3 - 2 * block)

    gap = place(source // depth) * depth + lax.rem(source, depth)
    gap = sign * (gap - place(1 + at // depth) * depth - lax.rem(at, depth))
    total = jnp.zeros(shape, jnp.float32)
    for tap in range(weight.shape[0]):
        total = total + jnp.where(gap == offset[tap], weight[tap], 0.0)
    total = jnp.where(same_row(shape), total, 0.0)
    high = total.astype(jnp.bfloat16)
    low = (total - high.astype(jnp.float32)).astype(jnp.bfloat16)
    half = depth * ROWS
    sides = [piece[o * half : (o + 1) * half] for o in range(2) for piece in (high, low)]
    return jnp.concatenate(sides, axis=0)


def both_parts(sums, half):
    return sums[:half] + sums[half : 2 * half]


def exchange_kernel(
    sizes, est, obs, weight, offset, shot, gain, fit, out, final,
    fit_kept, est_kept, obs_kept, est_got, obs_got, far_a, far_b, res, band, band_back, fit_wide, own,
    part_out, part_in, coef, coef_a, coef_b, mine, other, returned,
    load_sem, store_sem, pair_sem, far_sem, part_sem, edge_sem, back_sem, ret_sem,
):
    parts, slabs, chunks, dirs, depth, width, share = sizes
    slab = lax.axis_index("gz").astype(jnp.int32)
    part = lax.axis_index("dir").astype(jnp.int32)
    odd = lax.rem(slab, 2)
    partner = slab + 1 - 2 * odd
    away = slab - 2 + 4 * odd
    across = slab + 2 - 4 * odd
    has_away = jnp.logical_and(away >= 0, away < slabs)
    has_across = jnp.logical_and(across >= 0, across < slabs)
    cuts = divisor(dirs // 2, CUTS)
    some = dirs // cuts
    span = share * ROWS
    count = divisor(share // 2, PIECES)
    step = span // count
    pair_rows = 2 * ROWS
    half = depth * ROWS

    def part_of(hop):
        return lax.rem(part + hop, parts)

    barrier = pltpu.get_barrier_semaphore()

    def greet(name, index):
        pl.semaphore_signal(barrier, inc=1, device_id={name: index}, device_id_type=MESH)

    greet("gz", partner)
    for hop in range(1, parts):
        greet("dir", part_of(hop))

    @pl.when(has_away)
    def _():
        greet("gz", away)

    @pl.when(has_across)
    def _():
        greet("gz", across)

    pl.semaphore_wait(barrier, parts + has_away.astype(jnp.int32) + has_across.astype(jnp.int32))

    def remote(source, target, sems, name, index):
        return pltpu.make_async_remote_copy(
            src_ref=source, dst_ref=target, send_sem=sems.at[0], recv_sem=sems.at[1],
            device_id={name: index}, device_id_type=MESH,
        )

    def rows_at(side, chunk):
        return pl.ds(pl.multiple_of((side * chunks + chunk) * ROWS, ROWS), ROWS)

    def cut_of(cut):
        return pl.ds(cut * some, some)

    def piece(i):
        return pl.ds(i * step, step)

    def pair_copy(kind, chunk, cut):
        source, target = ((est, est_got), (obs, obs_got))[kind]
        return remote(
            source.at[cut_of(cut), :, rows_at(1 - odd, chunk), :],
            target.at[chunk, cut_of(cut)],
            pair_sem.at[kind, chunk, cut], "gz", partner,
        )

    def away_copy(chunk, cut):
        return remote(
            est.at[cut_of(cut), :, rows_at(odd, chunk), :],
            far_a.at[chunk, cut_of(cut)],
            far_sem.at[0, chunk, cut], "gz", away,
        )

    def across_copy(chunk, cut):
        return remote(
            est_got.at[chunk, cut_of(cut)], far_b.at[chunk, cut_of(cut)],
            far_sem.at[1, chunk, cut], "gz", across,
        )

    def load_copy(kind, chunk):
        source, target = ((est, est_kept), (obs, obs_kept))[kind]
        return pltpu.make_async_copy(
            source.at[:, :, rows_at(odd, chunk), :], target.at[chunk], load_sem.at[kind, chunk]
        )

    def part_copy(o, chunk, hop, i):
        at = (chunk, hop - 1, pl.ds(o * depth, depth), piece(i))
        return remote(
            part_out.at[at], part_in.at[at], part_sem.at[o, chunk, hop - 1, i], "dir", part_of(hop)
        )

    def edge_copy(kind, chunk, i):
        target, index = ((coef_a, away), (coef_b, across))[kind]
        return remote(
            coef.at[chunk, pl.ds(kind * depth, depth), piece(i), :],
            target.at[chunk, :, piece(i), :],
            edge_sem.at[kind, chunk, i], "gz", index,
        )

    def back_copy(chunk, i):
        return remote(
            other.at[chunk, :, piece(i), :], returned.at[chunk, :, piece(i), :],
            back_sem.at[chunk, i], "gz", partner,
        )

    def tile_of(kind, chunk):
        side = odd if kind == 0 else 1 - odd
        return side * chunks + chunk

    def ret_copy(kind, chunk, hop, i):
        source = (mine, returned)[kind]
        return remote(
            source.at[chunk, :, piece(i), :], out.at[tile_of(kind, chunk), part, :, piece(i), :],
            ret_sem.at[kind, chunk, hop - 1, i], "dir", part_of(hop),
        )

    def store_copy(kind, chunk):
        if kind and chunk == chunks - 1:
            return pltpu.make_async_copy(returned.at[chunk], final, store_sem.at[kind, chunk])
        source = (mine, returned)[kind]
        return pltpu.make_async_copy(
            source.at[chunk], out.at[tile_of(kind, chunk), part], store_sem.at[kind, chunk]
        )

    def begin(chunk):
        for kind in range(2):
            for cut in range(cuts):
                pair_copy(kind, chunk, cut).start()

        @pl.when(has_away)
        def _():
            for cut in range(cuts):
                away_copy(chunk, cut).start()

        for kind in range(2):
            load_copy(kind, chunk).start()

    def forward(chunk, cut):
        pair_copy(0, chunk, cut).wait_recv()

        @pl.when(has_across)
        def _():
            across_copy(chunk, cut).start()

    def arrive(near, far):
        @pl.when(has_across)
        def _():
            near.wait_recv()

        @pl.when(has_away)
        def _():
            far.wait_recv()

    shots = [shot[lax.div(index * depth, SLAB)] for index in (slab, partner)]

    def residual(o, chunk, cut):
        if o:
            pair_copy(1, chunk, cut).wait_recv()
        else:
            arrive(away_copy(chunk, cut), across_copy(chunk, cut))
        seen = (obs_kept, obs_got)[o]

        def one(j, carry):
            d = cut * some + 2 * j
            columns = []
            for e in range(2):
                planes = [
                    ref[chunk, d + e].astype(jnp.float32).reshape(half, width)
                    for ref in (far_b, est_kept, est_got, far_a)
                ]
                columns.append(jnp.concatenate(planes, axis=0))
            wide = jnp.concatenate(columns, axis=1).astype(jnp.bfloat16)
            rows = band[2 * o * half : 2 * (o + 1) * half, :]
            sums = both_parts(jnp.dot(rows, wide, preferred_element_type=jnp.float32), half)
            values = []
            for e in range(2):
                scale = gain[shots[o], d + e]
                value = seen[chunk, d + e].astype(jnp.float32).reshape(half, width)
                value = value - scale * sums[:, e * width : (e + 1) * width]
                values.append(scale * value)
            at = pl.ds(pl.multiple_of(d * ROWS, pair_rows), pair_rows)
            for z in range(depth):
                cut_rows = slice(z * ROWS, (z + 1) * ROWS)
                both = jnp.concatenate([value[cut_rows] for value in values], axis=0)
                res[o * depth + z, at, :] = both.astype(jnp.bfloat16)
            return carry

        lax.fori_loop(0, some // 2, one, 0)

    def fitting(o, chunk):
        def one(j, carry):
            z = o * depth + 2 * j
            wide = jnp.concatenate([res[z], res[z + 1]], axis=1)
            made = jnp.dot(fit_wide[...], wide, preferred_element_type=jnp.float32)
            for e in range(2):
                value = made[:, e * width : (e + 1) * width]
                own[z + e] = value[:span]
                for hop in range(1, parts):
                    piece_of = value[hop * span : (hop + 1) * span]
                    part_out[chunk, hop - 1, z + e] = piece_of.astype(jnp.bfloat16)
            return carry

        lax.fori_loop(0, depth // 2, one, 0)
        for i in range(count):
            for hop in range(1, parts):
                part_copy(o, chunk, hop, i).start()

    def gather(o, chunk, i):
        for hop in range(1, parts):
            part_copy(o, chunk, hop, i).wait_recv()

        def one(z, carry):
            value = own[z, piece(i), :]
            for hop in range(1, parts):
                value = value + part_in[chunk, hop - 1, z, piece(i), :].astype(jnp.float32)
            coef[chunk, z, piece(i), :] = value.astype(jnp.bfloat16)
            return carry

        lax.fori_loop(o * depth, (o + 1) * depth, one, 0)

        @pl.when((has_away, has_across)[o])
        def _():
            edge_copy(o, chunk, i).start()

    def smooth(chunk, i):
        arrive(edge_copy(0, chunk, i), edge_copy(1, chunk, i))

        def one(j, carry):
            at = pl.ds(pl.multiple_of(i * step + j * pair_rows, pair_rows), pair_rows)
            planes = [coef_b[chunk, z, at, :] for z in range(depth)]
            planes += [coef[chunk, z, at, :] for z in range(2 * depth)]
            planes += [coef_a[chunk, z, at, :] for z in range(depth)]
            planes = [plane.astype(jnp.float32) for plane in planes]
            columns = [
                jnp.concatenate([plane[e * ROWS : (e + 1) * ROWS] for plane in planes], axis=0)
                for e in range(2)
            ]
            wide = jnp.concatenate(columns, axis=1).astype(jnp.bfloat16)
            sums = jnp.dot(band_back[...], wide, preferred_element_type=jnp.float32)
            for o, ref in enumerate((mine, other)):
                side = both_parts(sums[2 * o * half : 2 * (o + 1) * half], half)
                for z in range(depth):
                    value = side[z * ROWS : (z + 1) * ROWS]
                    both = jnp.concatenate([value[:, :width], value[:, width:]], axis=0)
                    ref[chunk, z, at, :] = both.astype(jnp.bfloat16)
            return carry

        lax.fori_loop(0, step // pair_rows, one, 0)
        back_copy(chunk, i).start()
        for hop in range(1, parts):
            ret_copy(0, chunk, hop, i).start()

    def pass_on(chunk, i):
        back_copy(chunk, i).wait_recv()
        for hop in range(1, parts):
            if chunk < chunks - 1:
                ret_copy(1, chunk, hop, i).start()

    fit_copy = pltpu.make_async_copy(fit, fit_kept, load_sem.at[2, 0])
    fit_copy.start()
    begin(0)
    if chunks > 1:
        begin(1)

    nothing = jnp.zeros((dirs, depth, ROWS, width), jnp.bfloat16)
    no_coef = jnp.zeros((depth, span, width), jnp.bfloat16)

    def clear(ref, value):
        def one(chunk, carry):
            ref[chunk] = value
            return carry

        lax.fori_loop(0, chunks, one, 0)

    @pl.when(jnp.logical_not(has_across))
    def _():
        clear(far_a, nothing)
        clear(coef_a, no_coef)

    @pl.when(jnp.logical_not(has_away))
    def _():
        clear(far_b, nothing)
        clear(coef_b, no_coef)

    band[...] = band_matrix(weight, offset, odd, depth, 1)
    band_back[...] = band_matrix(weight, offset, odd, depth, -1)
    line = iota((parts * span, fit.shape[0]), 0) // ROWS
    chosen = lax.rem(line // share + part, parts) * share + lax.rem(line, share)
    spread = ones_where(chosen == iota(line.shape, 1))
    fit_copy.wait()
    narrow = jnp.dot(spread, fit_kept[...], preferred_element_type=jnp.float32).astype(jnp.bfloat16)
    shape = (dirs * ROWS, fit.shape[1])
    spread = ones_where(iota(shape, 0) // ROWS + part * dirs == iota(shape, 1))
    full = against(narrow, spread)
    fit_wide[...] = jnp.where(same_row(full.shape), full, 0.0).astype(jnp.bfloat16)

    for cut in range(cuts):
        forward(0, cut)
    for chunk in range(chunks):
        more = chunk + 1 < chunks
        for kind in range(2):
            load_copy(kind, chunk).wait()
        for cut in range(cuts):
            residual(0, chunk, cut)
        fitting(0, chunk)
        for cut in range(cuts):
            residual(1, chunk, cut)
        fitting(1, chunk)
        if chunk:
            for i in range(count):
                pass_on(chunk - 1, i)
            store_copy(1, chunk - 1).start()
        for i in range(count):
            gather(0, chunk, i)
        for i in range(count):
            gather(1, chunk, i)
            for cut in range(cuts):
                if more and cut * count // cuts == i:
                    forward(chunk + 1, cut)
            if i:
                smooth(chunk, i - 1)
            if not more and i > 1:
                pass_on(chunk, i - 2)
        smooth(chunk, count - 1)
        store_copy(0, chunk).start()
        if not more:
            for i in range(max(count - 2, 0), count):
                pass_on(chunk, i)
            store_copy(1, chunk).start()
        if chunk + 2 < chunks:
            begin(chunk + 2)

    for chunk in range(chunks):
        for cut in range(cuts):
            for kind in range(2):
                pair_copy(kind, chunk, cut).wait_send()

            @pl.when(has_away)
            def _(chunk=chunk, cut=cut):
                away_copy(chunk, cut).wait_send()

            @pl.when(has_across)
            def _(chunk=chunk, cut=cut):
                across_copy(chunk, cut).wait_send()

        for i in range(count):
            for hop in range(1, parts):
                for o in range(2):
                    part_copy(o, chunk, hop, i).wait_send()

            @pl.when(has_away)
            def _(chunk=chunk, i=i):
                edge_copy(0, chunk, i).wait_send()

            @pl.when(has_across)
            def _(chunk=chunk, i=i):
                edge_copy(1, chunk, i).wait_send()

            back_copy(chunk, i).wait_send()
            for kind in range(2):
                for hop in range(1, parts):
                    if kind == 0 or chunk < chunks - 1:
                        ret_copy(kind, chunk, hop, i).wait()
        for kind in range(2):
            store_copy(kind, chunk).wait()


def exchange_call(sizes, est, obs, weight, offset, shot, gain, fit):
    parts, slabs, chunks, dirs, depth, width, share = sizes
    span = share * ROWS
    count = divisor(share // 2, PIECES)
    cuts = divisor(dirs // 2, CUTS)
    bf16 = jnp.bfloat16
    field = pltpu.VMEM((chunks, dirs, depth, ROWS, width), bf16)
    hops = pltpu.VMEM((chunks, parts - 1, 2 * depth, span, width), bf16)
    edge = pltpu.VMEM((chunks, depth, span, width), bf16)
    square = pltpu.VMEM((4 * depth * ROWS, 4 * depth * ROWS), bf16)
    smem = pl.BlockSpec(memory_space=pltpu.SMEM)
    hbm = pl.BlockSpec(memory_space=pl.ANY)
    dma = pltpu.SemaphoreType.DMA
    return pl.pallas_call(
        functools.partial(exchange_kernel, sizes),
        in_specs=[hbm, hbm, smem, smem, smem, smem, hbm],
        out_specs=[hbm, hbm],
        out_shape=[
            jax.ShapeDtypeStruct((2 * chunks, parts, depth, span, width), bf16),
            jax.ShapeDtypeStruct((depth, span, width), bf16),
        ],
        scratch_shapes=[pltpu.VMEM(fit.shape[::-1], bf16)]
        + [field] * 6
        + [
            pltpu.VMEM((2 * depth, dirs * ROWS, width), bf16),
            square,
            square,
            pltpu.VMEM((parts * span, dirs * ROWS), bf16),
            pltpu.VMEM((2 * depth, span, width), jnp.float32),
            hops,
            hops,
            pltpu.VMEM((chunks, 2 * depth, span, width), bf16),
        ]
        + [edge] * 5
        + [
            dma((3, chunks)),
            dma((2, chunks)),
            dma((2, chunks, cuts, 2)),
            dma((2, chunks, cuts, 2)),
            dma((2, chunks, parts - 1, count, 2)),
            dma((2, chunks, count, 2)),
            dma((chunks, count, 2)),
            dma((2, chunks, parts - 1, count, 2)),
        ],
        compiler_params=pltpu.CompilerParams(
            collective_id=0, has_side_effects=True, vmem_limit_bytes=60 * 1024 * 1024
        ),
    )(est, obs, weight, offset, shot, gain, fit.T)


def synthesis_kernel(by_hop, filtered, estimate, basis, *refs):
    correction, updated, wide = refs[-3:]
    parts, depth, span, width = filtered.shape[-4:]
    dirs = estimate.shape[0]
    part = lax.axis_index("dir").astype(jnp.int32)

    @pl.when(pl.program_id(0) == 0)
    def _():
        shape = (dirs * ROWS, basis.shape[1])
        spread = ones_where(iota(shape, 0) // ROWS + part * dirs == iota(shape, 1))
        narrow = against(spread, basis[...]).astype(jnp.bfloat16)
        shape = (parts * span, basis.shape[0])
        line = iota(shape, 0) // ROWS
        if by_hop:
            share = span // ROWS
            line = lax.rem(part - line // share + parts, parts) * share + lax.rem(line, share)
        spread = ones_where(line == iota(shape, 1))
        full = against(narrow, spread)
        wide[...] = jnp.where(same_row(full.shape), full, 0.0).astype(jnp.bfloat16)

    def one(j, carry):
        z = 2 * j
        columns = [
            jnp.concatenate([filtered[0, p, z + e] for p in range(parts)], axis=0) for e in range(2)
        ]
        made = jnp.dot(
            wide[...], jnp.concatenate(columns, axis=1), preferred_element_type=jnp.float32
        )
        for e in range(2):
            value = made[:, e * width : (e + 1) * width].reshape(dirs, ROWS, width)
            value = value.astype(jnp.bfloat16)
            correction[:, z + e] = value
            updated[:, z + e] = (
                estimate[:, z + e].astype(jnp.float32) + STEP_SIZE * value.astype(jnp.float32)
            ).astype(updated.dtype)
        return carry

    lax.fori_loop(0, depth // 2, one, 0)


def final_kernel(*refs):
    pieces, rest = refs[: -8], refs[-8:]
    estimate, basis, _, _, correction, updated, wide, joined = rest
    for number, piece in enumerate(pieces):
        joined[0, number] = piece[...]
    synthesis_kernel(True, joined, estimate, basis, correction, updated, wide)


def final_tile(tiles):
    odd = lax.rem(lax.axis_index("gz").astype(jnp.int32), 2)
    return (1 - odd) * (tiles // 2) + tiles // 2 - 1


def synthesis_call(filtered, estimate, basis):
    tiles, parts, depth, span, width = filtered.shape
    dirs = estimate.shape[0]

    def tile(i):
        return i + (i >= final_tile(tiles)).astype(jnp.int32)

    place = pl.BlockSpec((dirs, depth, ROWS, width), lambda i: (0, 0, tile(i), 0))
    shape = jax.ShapeDtypeStruct(estimate.shape, estimate.dtype)
    return pl.pallas_call(
        functools.partial(synthesis_kernel, False),
        grid=(tiles - 1,),
        in_specs=[
            pl.BlockSpec((1, parts, depth, span, width), lambda i: (tile(i), 0, 0, 0, 0)),
            place,
            pl.BlockSpec(basis.shape, lambda i: (0, 0)),
        ],
        out_specs=[place, place],
        out_shape=[shape, shape],
        scratch_shapes=[pltpu.VMEM((dirs * ROWS, parts * span), jnp.bfloat16)],
        cost_estimate=pl.CostEstimate(
            flops=2 * parts * span * estimate.size, bytes_accessed=8 * estimate.size, transcendentals=0
        ),
    )(filtered, estimate, basis)


def final_call(pieces, estimate, basis, made, tiles):
    depth, span, width = pieces[0].shape
    dirs = estimate.shape[0]
    place = pl.BlockSpec((dirs, depth, ROWS, width), lambda i: (0, 0, final_tile(tiles), 0))
    shape = jax.ShapeDtypeStruct(estimate.shape, estimate.dtype)
    parts = len(pieces)
    hbm = pl.BlockSpec(memory_space=pl.ANY)
    return pl.pallas_call(
        final_kernel,
        grid=(1,),
        in_specs=[pl.BlockSpec(pieces[0].shape, lambda i: (0, 0, 0))] * parts
        + [place, pl.BlockSpec(basis.shape, lambda i: (0, 0)), hbm, hbm],
        out_specs=[place, place],
        out_shape=[shape, shape],
        scratch_shapes=[
            pltpu.VMEM((dirs * ROWS, parts * span), jnp.bfloat16),
            pltpu.VMEM((1, parts, depth, span, width), jnp.bfloat16),
        ],
        input_output_aliases={parts + 2: 0, parts + 3: 1},
    )(*pieces, estimate, basis, *made)


def shards(
    estimate, observed, profile_weight, band_offset, slab_shot, shot_gain, fit_matrix, basis
):
    dirs, depth, rows, width = estimate.shape
    parts = lax.axis_size("dir")
    share = 2 * -(-fit_matrix.shape[1] // (2 * parts))
    sizes = (parts, lax.axis_size("gz"), rows // (2 * ROWS), dirs, depth, width, share)
    filtered, last = exchange_call(
        sizes, estimate, observed, profile_weight, band_offset, slab_shot, shot_gain, fit_matrix
    )
    pieces = [last] + [
        lax.ppermute(last, "dir", [(i, (i + hop) % parts) for i in range(parts)])
        for hop in range(1, parts)
    ]
    made = synthesis_call(filtered, estimate, basis)
    return tuple(final_call(pieces, estimate, basis, made, filtered.shape[0]))


def solution(mesh):
    return jax.shard_map(
        shards,
        mesh=mesh,
        in_specs=(
            P("dir", "gz", "gy", None),
            P("dir", "gz", "gy", None),
            P(),
            P(),
            P(),
            P(None, "dir"),
            P(),
            P(),
        ),
        out_specs=(P("dir", "gz", "gy", None), P("dir", "gz", "gy", None)),
        check_vma=False,
    )
```
